32 devices in a mesh: groups: 2 (over y), seq: 4 (over z), heads: 4 (over x, core).
Axes of the slice: x: 2, y: 2, z: 4, core: 2. Of those that a mesh axis runs over, the one named last changes fastest.
Arguments:
- queries: bfloat16 [4096, 24, 128], P(('groups', 'seq'), 'heads'), parts along dimension 0, may hold values from -130 to 130
- keys: bfloat16 [4096, 24, 128], P(('groups', 'seq'), 'heads'), parts along dimension 0, may hold values from -6 to 6
- values: bfloat16 [4096, 24, 128], P(('groups', 'seq'), 'heads'), parts along dimension 0, may hold values from -6 to 6
- pool_keys: bfloat16 [24, 8, 128], P('heads'), may hold values from -0.5 to 0.5
- pool_values: bfloat16 [24, 8, 128], P('heads'), may hold values from -0.5 to 0.5
Outputs:
- attended: bfloat16 [4096, 24, 128], P(('groups', 'seq'), 'heads'), parts along dimension 0
The draws below stay inside these ranges and needn't reach their ends.
There are 2 independent parts, one for each index of `groups`. The reference program is written for one: setup_inputs(seed, part) draws one part's arguments, and reference() takes and returns one part's arrays. A program takes and returns all parts, laid end to end along the dimension named above; an argument that names none is the same for every part. Nothing has to cross between parts.
All inputs are finite; a program needn't handle non-finite values.
Results may differ from the reference program's by a relative error of at most 0.01.
Values may be sent and summed in bfloat16 or wider, within the bound.
A program may use at most 64 MiB of HBM per device.

```python
import jax
import jax.numpy as jnp
from jax import lax

HD = 128
HEADS = 24
BLOCK = 128
SUMS = 8
TOKENS = 2048


def common_rows(key):
    base_keys = jnp.clip(jax.random.normal(jax.random.fold_in(key, 11), (TOKENS, HEADS, HD), jnp.float32), -6.0, 6.0)
    base_queries = jnp.clip(2.5 * jax.random.normal(jax.random.fold_in(key, 12), (TOKENS, HEADS, HD), jnp.float32), -15.0, 15.0)
    return (base_keys, base_queries)


def draw_keys(key, part):
    base_keys, base_queries = common_rows(key)
    return base_keys.astype(jnp.bfloat16)


def draw_queries(key, part):
    base_keys, base_queries = common_rows(key)
    return base_queries.astype(jnp.bfloat16)


def block_levels(key, dims, shards, smallest, top_value):
    gain = 1.0
    for position, shards_of in shards:
        draws = jax.random.uniform(jax.random.fold_in(jax.random.fold_in(key, 6), position), (shards_of,), jnp.float32, smallest / len(shards), top_value / len(shards))
        gain = gain * jnp.repeat(jnp.exp(draws), dims[position] // shards_of).reshape((-1,) + (1,) * (len(dims) - 1 - position))
    return gain


def normal_values(key, dims, width, reach, shards=(), kind=jnp.bfloat16):
    drawn = width * jax.random.normal(key, dims, jnp.float32)
    if shards:
        drawn = drawn * block_levels(key, dims, shards, -0.22, 0.18)
    return jnp.clip(drawn, -reach, reach).astype(kind)


def setup_inputs(seed: int = 0, part: int = 0) -> dict:
    key_list = jax.random.split(jax.random.key(seed), 6)
    own_keys = jax.random.split(jax.random.fold_in(key_list[5], part), 6)
    queries = draw_queries(jax.random.fold_in(jax.random.fold_in(key_list[5], part), 71), part)
    keys = draw_keys(jax.random.fold_in(jax.random.fold_in(key_list[5], part), 71), part)
    values = normal_values(own_keys[2], (TOKENS, HEADS, HD), 1.0, 6.0, ((0, 4), (1, 4)))
    pool_keys = normal_values(key_list[3], (HEADS, SUMS, BLOCK), BLOCK ** -0.5, 0.5, ((0, 4),))
    pool_values = normal_values(key_list[4], (HEADS, SUMS, BLOCK), BLOCK ** -0.5, 0.5, ((0, 4),))
    return {"queries": queries, "keys": keys, "values": values, "pool_keys": pool_keys, "pool_values": pool_values}


NEG = -1.0e30


def reference(queries, keys, values, pool_keys, pool_values):
    blocks = TOKENS // BLOCK
    logit_scale = HD ** -0.5
    key_blocks = keys.reshape(blocks, BLOCK, HEADS, HD).astype(jnp.float32)
    value_blocks = values.reshape(blocks, BLOCK, HEADS, HD).astype(jnp.float32)
    summary_keys = jnp.einsum("hsb,nbhd->nshd", pool_keys.astype(jnp.float32), key_blocks).astype(jnp.bfloat16).reshape(blocks * SUMS, HEADS, HD)
    summary_values = jnp.einsum("hsb,nbhd->nshd", pool_values.astype(jnp.float32), value_blocks).astype(jnp.bfloat16).reshape(blocks * SUMS, HEADS, HD)
    positions = jnp.arange(TOKENS, dtype=jnp.int32)
    query_block = positions // BLOCK
    row_block = jnp.arange(blocks * SUMS, dtype=jnp.int32) // SUMS
    summary_mask = row_block[None, :] < query_block[:, None]
    inner = jnp.arange(BLOCK, dtype=jnp.int32)[:, None]
    outer = jnp.arange(2 * BLOCK, dtype=jnp.int32)[None, :]
    block_index = jnp.arange(blocks, dtype=jnp.int32)[:, None, None]
    window_mask = ((outer > inner) & (outer <= inner + BLOCK))[None] & (block_index * BLOCK + outer[None] - BLOCK >= 0)

    def one_head(input_arrays):
        query_matrix, key_row_slab, value_row_slab, summary_key_rows, summary_value_rows = input_arrays
        padding = jnp.zeros((BLOCK, HD), jnp.bfloat16)
        key_ext = jnp.concatenate([padding, key_row_slab], axis=0).reshape(blocks + 1, BLOCK, HD)
        value_ext = jnp.concatenate([padding, value_row_slab], axis=0).reshape(blocks + 1, BLOCK, HD)
        key_win = jnp.concatenate([key_ext[:-1], key_ext[1:]], axis=1)
        value_win = jnp.concatenate([value_ext[:-1], value_ext[1:]], axis=1)
        query_blocks = query_matrix.reshape(blocks, BLOCK, HD)
        window_scores = jnp.einsum("nid,njd->nij", query_blocks.astype(jnp.float32), key_win.astype(jnp.float32)) * logit_scale
        window_scores = jnp.where(window_mask, window_scores, NEG)
        summary_logits = jnp.dot(query_matrix, summary_key_rows.T, preferred_element_type=jnp.float32) * logit_scale
        summary_logits = jnp.where(summary_mask, summary_logits, NEG)
        top = jnp.maximum(window_scores.max(-1).reshape(TOKENS), summary_logits.max(-1))
        window_weights = jnp.where(window_mask, jnp.exp(window_scores - top.reshape(blocks, BLOCK, 1)), 0.0)
        summary_weights = jnp.where(summary_mask, jnp.exp(summary_logits - top[:, None]), 0.0)
        total = window_weights.sum(-1).reshape(TOKENS) + summary_weights.sum(-1)
        window_b = lax.optimization_barrier(window_weights.astype(jnp.bfloat16))
        window_part = jnp.einsum("nij,njd->nid", window_b.astype(jnp.float32), value_win.astype(jnp.float32)).reshape(TOKENS, HD)
        summary_part = jnp.dot(summary_weights.astype(jnp.bfloat16), summary_value_rows, preferred_element_type=jnp.float32)
        return ((window_part + summary_part) / total[:, None]).astype(jnp.bfloat16)

    result = lax.map(one_head, (jnp.moveaxis(queries, 1, 0), jnp.moveaxis(keys, 1, 0), jnp.moveaxis(values, 1, 0), jnp.moveaxis(summary_keys, 1, 0), jnp.moveaxis(summary_values, 1, 0)))
    return jnp.moveaxis(result, 0, 1)
```

```python
import functools
import math

import jax
import jax.numpy as jnp
from jax import lax
from jax.experimental import pallas as pl
from jax.experimental.pallas import tpu as pltpu
from jax.sharding import PartitionSpec as P

NEG = -1e30
F32 = jnp.float32
BF16 = jnp.bfloat16


def dot_t(a, b):
    return lax.dot_general(a, b, (((1,), (1,)), ((), ())), preferred_element_type=F32)


def dot(a, b):
    return jnp.dot(a, b, preferred_element_type=F32)


def kernel(
    peers, q_hbm, k_hbm, v_hbm, pk_ref, pv_ref, o_hbm,
    q_buf, k_buf, v_buf, o_buf, prev, summ, top_s, total_s, acc_s,
    in_sem, out_sem, prev_send, prev_recv, sum_send, sum_recv,
):
    heads, rows, width = q_buf.shape
    sums, block = pk_ref.shape[1], pk_ref.shape[2]
    blocks = rows // block
    own = blocks * sums
    gain = (width ** -0.5) * math.log2(math.e)
    spot = lax.axis_index("seq")

    k_in = pltpu.make_async_copy(k_hbm, k_buf, in_sem.at[0])
    v_in = pltpu.make_async_copy(v_hbm, v_buf, in_sem.at[1])
    q_in = pltpu.make_async_copy(q_hbm, q_buf, in_sem.at[2])
    k_in.start()
    v_in.start()
    q_in.start()

    barrier = pltpu.get_barrier_semaphore()

    def greet(i, c):
        pl.semaphore_signal(
            barrier, inc=1, device_id={"seq": i}, device_id_type=pl.DeviceIdType.MESH
        )
        return c

    lax.fori_loop(0, spot, greet, 0)

    def clear(i, c):
        summ[i] = jnp.zeros(summ.shape[1:], BF16)
        return c

    lax.fori_loop(spot + 1, summ.shape[0], clear, 0)

    @pl.when(spot == 0)
    def _():
        prev[...] = jnp.zeros(prev.shape, BF16)

    @pl.when(spot < peers - 1)
    def _():
        pl.semaphore_wait(barrier, peers - 1 - spot)

    def prev_copy(i, ref, to):
        return pltpu.make_async_remote_copy(
            src_ref=ref.at[:, pl.ds(rows - block, block), :],
            dst_ref=prev.at[i],
            send_sem=prev_send.at[i],
            recv_sem=prev_recv.at[i],
            device_id={"seq": to},
            device_id_type=pl.DeviceIdType.MESH,
        )

    @pl.when(spot < peers - 1)
    def _():
        prev_copy(0, k_hbm, spot + 1).start()
        prev_copy(1, v_hbm, spot + 1).start()

    row_group = lax.broadcasted_iota(jnp.int32, (own, block), 0) // sums

    def summarise(which, pool_ref, buf, h):
        pool = pool_ref[h].astype(F32)
        tall = jnp.concatenate([pool] * blocks, axis=0)
        wide = jnp.concatenate(
            [jnp.where(row_group == b, tall, 0.0) for b in range(blocks)], axis=1
        ).astype(BF16)
        summ[spot, which, h] = dot(wide, buf[h]).astype(BF16)

    k_in.wait()
    for h in range(heads):
        summarise(0, pk_ref, k_buf, h)
    v_in.wait()
    for h in range(heads):
        summarise(1, pv_ref, v_buf, h)

    def sum_copy(source, to):
        return pltpu.make_async_remote_copy(
            src_ref=summ.at[source],
            dst_ref=summ.at[source],
            send_sem=sum_send.at[to],
            recv_sem=sum_recv.at[source],
            device_id={"seq": to},
            device_id_type=pl.DeviceIdType.MESH,
        )

    def send(i, c):
        sum_copy(spot, i).start()
        return c

    lax.fori_loop(spot + 1, peers, send, 0)
    q_in.wait()

    r = lax.broadcasted_iota(jnp.int32, (block, block), 0)
    c = lax.broadcasted_iota(jnp.int32, (block, block), 1)
    lower = c <= r

    def window(scores, v_now, v_before):
        top = jnp.max(scores, axis=1, keepdims=True)
        weights = jnp.exp2((scores - top) * gain)
        total = jnp.sum(weights, axis=1, keepdims=True)
        near = jnp.where(lower, weights, 0.0).astype(BF16)
        far = jnp.where(lower, 0.0, weights).astype(BF16)
        return top, total, dot(near, v_now) + dot(far, v_before)

    def keep(h, b, top, total, acc):
        at = pl.ds(b * block, block)
        top_s[h, at, :] = jnp.broadcast_to(top, (block, width))
        total_s[h, at, :] = jnp.broadcast_to(total, (block, width))
        acc_s[h, at, :] = acc

    def near_head(h, carry):
        for b in range(1, blocks):
            now, before = pl.ds(b * block, block), pl.ds((b - 1) * block, block)
            q = q_buf[h, now, :]
            scores = jnp.where(lower, dot_t(q, k_buf[h, now, :]), dot_t(q, k_buf[h, before, :]))
            keep(h, b, *window(scores, v_buf[h, now, :], v_buf[h, before, :]))
        return carry

    lax.fori_loop(0, heads, near_head, 0)

    @pl.when(spot > 0)
    def _():
        prev_copy(0, k_hbm, spot).wait_recv()
        prev_copy(1, v_hbm, spot).wait_recv()

    def land(i, c):
        sum_copy(i, spot).wait_recv()
        return c

    lax.fori_loop(0, spot, land, 0)

    per = block // own
    seen = (lower | (spot > 0))

    def o_copy(h):
        return pltpu.make_async_copy(o_buf.at[h], o_hbm.at[h], out_sem.at[h])

    def far_head(h, carry):
        now = pl.ds(0, block)
        q = q_buf[h, now, :]
        scores = jnp.where(lower, dot_t(q, k_buf[h, now, :]), dot_t(q, prev[0, h]))
        scores = jnp.where(seen, scores, NEG)
        keep(h, 0, *window(scores, v_buf[h, now, :], prev[1, h]))

        def chunk(j, carry):
            keys = jnp.concatenate([summ[j * per + i, 0, h] for i in range(per)], axis=0)
            values = jnp.concatenate([summ[j * per + i, 1, h] for i in range(per)], axis=0)
            for b in range(blocks):
                at = pl.ds(b * block, block)
                row_block = j * (block // sums) + c // sums
                scores = dot_t(q_buf[h, at, :], keys)
                scores = jnp.where(row_block < spot * blocks + b, scores, NEG)
                old = top_s[h, at, :]
                top = jnp.maximum(old, jnp.max(scores, axis=1, keepdims=True))
                weights = jnp.exp2((scores - top) * gain)
                fade = jnp.exp2((old - top) * gain)
                top_s[h, at, :] = top
                total_s[h, at, :] = total_s[h, at, :] * fade + jnp.sum(
                    weights, axis=1, keepdims=True
                )
                acc_s[h, at, :] = acc_s[h, at, :] * fade + dot(weights.astype(BF16), values)
            return carry

        chunks = summ.shape[0] // per
        if chunks == 1:
            chunk(0, 0)
        else:
            lax.fori_loop(0, (spot * own + own - sums + block - 1) // block, chunk, 0)
        o_buf[h] = (acc_s[h] / total_s[h]).astype(BF16)
        o_copy(h).start()
        return carry

    lax.fori_loop(0, heads, far_head, 0)

    @pl.when(spot < peers - 1)
    def _():
        prev_copy(0, k_hbm, spot + 1).wait_send()
        prev_copy(1, v_hbm, spot + 1).wait_send()

    def sent(i, c):
        sum_copy(spot, i).wait_send()
        return c

    lax.fori_loop(spot + 1, peers, sent, 0)
    for h in range(heads):
        o_copy(h).wait()


def on_device(peers, queries, keys, values, pool_keys, pool_values):
    rows, heads, width = queries.shape
    sums, block = pool_keys.shape[1], pool_keys.shape[2]
    own = rows // block * sums
    per = block // own
    slots = -(-peers // per) * per
    q, k, v = (jnp.moveaxis(x, 1, 0) for x in (queries, keys, values))
    hbm = pl.BlockSpec(memory_space=pl.ANY)
    vmem = pl.BlockSpec(memory_space=pltpu.VMEM)
    out = pl.pallas_call(
        functools.partial(kernel, peers),
        out_shape=jax.ShapeDtypeStruct((heads, rows, width), BF16),
        in_specs=[hbm, hbm, hbm, vmem, vmem],
        out_specs=hbm,
        scratch_shapes=[
            pltpu.VMEM((heads, rows, width), BF16),
            pltpu.VMEM((heads, rows, width), BF16),
            pltpu.VMEM((heads, rows, width), BF16),
            pltpu.VMEM((heads, rows, width), BF16),
            pltpu.VMEM((2, heads, block, width), BF16),
            pltpu.VMEM((slots, 2, heads, own, width), BF16),
            pltpu.VMEM((heads, rows, width), F32),
            pltpu.VMEM((heads, rows, width), F32),
            pltpu.VMEM((heads, rows, width), F32),
            pltpu.SemaphoreType.DMA((3,)),
            pltpu.SemaphoreType.DMA((heads,)),
            pltpu.SemaphoreType.DMA((2,)),
            pltpu.SemaphoreType.DMA((2,)),
            pltpu.SemaphoreType.DMA((peers,)),
            pltpu.SemaphoreType.DMA((peers,)),
        ],
        compiler_params=pltpu.CompilerParams(
            collective_id=0, has_side_effects=True, vmem_limit_bytes=40 * 1024 * 1024
        ),
    )(q, k, v, pool_keys, pool_values)
    return jnp.moveaxis(out, 0, 1)


def solution(mesh):
    in_specs = (
        P(("groups", "seq"), "heads", None),
        P(("groups", "seq"), "heads", None),
        P(("groups", "seq"), "heads", None),
        P("heads", None, None),
        P("heads", None, None),
    )
    out_specs = P(("groups", "seq"), "heads", None)
    return jax.shard_map(
        functools.partial(on_device, mesh.shape["seq"]),
        mesh=mesh, in_specs=in_specs, out_specs=out_specs, check_vma=False,
    )
```

```python
import functools
import math

import jax
import jax.numpy as jnp
from jax import lax
from jax.experimental import pallas as pl
from jax.experimental.pallas import tpu as pltpu
from jax.sharding import PartitionSpec as P

NEG = -1e30
F32 = jnp.float32
BF16 = jnp.bfloat16


def dot_t(a, b):
    return lax.dot_general(a, b, (((1,), (1,)), ((), ())), preferred_element_type=F32)


def dot(a, b):
    return jnp.dot(a, b, preferred_element_type=F32)


def kernel(
    peers, q_hbm, k_hbm, v_hbm, pk_hbm, pv_hbm, o_hbm,
    q_buf, k_buf, v_buf, pk_ref, pv_ref, o_buf, asked, answer, back, stat, stat_back,
    summ, top_s, total_s, acc_s,
    in_sem, out_sem, ask_send, ask_recv, back_send, back_recv, stat_sem, sum_send, sum_recv,
):
    heads, rows, width = q_buf.shape
    sums, block = pk_ref.shape[1], pk_ref.shape[2]
    blocks = rows // block
    own = blocks * sums
    gain = (width ** -0.5) * math.log2(math.e)
    spot = lax.axis_index("seq")
    slab = stat.shape[0] // 2

    k_in = pltpu.make_async_copy(k_hbm, k_buf, in_sem.at[0])
    v_in = pltpu.make_async_copy(v_hbm, v_buf, in_sem.at[1])
    q_in = pltpu.make_async_copy(q_hbm, q_buf, in_sem.at[2])
    k_in.start()
    v_in.start()
    q_in.start()
    pk_in = pltpu.make_async_copy(pk_hbm, pk_ref, in_sem.at[3])
    pv_in = pltpu.make_async_copy(pv_hbm, pv_ref, in_sem.at[4])
    pk_in.start()
    pv_in.start()

    barrier = pltpu.get_barrier_semaphore()

    def greet(i, c):
        pl.semaphore_signal(
            barrier, inc=1, device_id={"seq": i}, device_id_type=pl.DeviceIdType.MESH
        )
        return c

    lax.fori_loop(0, spot, greet, 0)

    @pl.when(spot < peers - 1)
    def _():
        greet(spot + 1, 0)

    def clear(i, c):
        summ[i] = jnp.zeros(summ.shape[1:], BF16)
        return c

    lax.fori_loop(spot + 1, summ.shape[0], clear, 0)

    @pl.when(spot == 0)
    def _():
        back[...] = jnp.zeros(back.shape, BF16)
        half = lax.broadcasted_iota(jnp.int32, stat_back.shape, 0) < slab
        stat_back[...] = jnp.where(half, NEG, 0.0)

    pl.semaphore_wait(barrier, peers - 1 - spot + jnp.where(spot > 0, 1, 0))

    def remote(src, dst, send_sem, recv_sem, to):
        return pltpu.make_async_remote_copy(
            src_ref=src,
            dst_ref=dst,
            send_sem=send_sem,
            recv_sem=recv_sem,
            device_id={"seq": to},
            device_id_type=pl.DeviceIdType.MESH,
        )

    def ask(h, to):
        src = q_hbm.at[h, pl.ds(0, block), :]
        return remote(src, asked.at[h], ask_send.at[h], ask_recv.at[h], to)

    def give(h, to):
        return remote(answer.at[h], back.at[h], back_send.at[h], back_recv.at[h], to)

    def give_stat(to):
        return remote(stat, stat_back, stat_sem.at[0], stat_sem.at[1], to)

    @pl.when(spot > 0)
    def _():
        for h in range(heads):
            ask(h, spot - 1).start()

    row_group = lax.broadcasted_iota(jnp.int32, (own, block), 0) // sums

    def summarise(which, pool_ref, buf, h):
        pool = pool_ref[h].astype(F32)
        tall = jnp.concatenate([pool] * blocks, axis=0)
        wide = jnp.concatenate(
            [jnp.where(row_group == b, tall, 0.0) for b in range(blocks)], axis=1
        ).astype(BF16)
        summ[spot, which, h] = dot(wide, buf[h]).astype(BF16)

    k_in.wait()
    pk_in.wait()
    for h in range(heads):
        summarise(0, pk_ref, k_buf, h)
    v_in.wait()
    pv_in.wait()
    for h in range(heads):
        summarise(1, pv_ref, v_buf, h)

    def sum_copy(source, to):
        return remote(summ.at[source], summ.at[source], sum_send.at[to], sum_recv.at[source], to)

    def send(i, c):
        sum_copy(spot, i).start()
        return c

    lax.fori_loop(spot + 1, peers, send, 0)
    q_in.wait()

    r = lax.broadcasted_iota(jnp.int32, (block, block), 0)
    c = lax.broadcasted_iota(jnp.int32, (block, block), 1)
    lower = c <= r

    def window(scores, v_now, v_before):
        top = jnp.max(scores, axis=1, keepdims=True)
        weights = jnp.exp2((scores - top) * gain)
        total = jnp.sum(weights, axis=1, keepdims=True)
        near = jnp.where(lower, weights, 0.0).astype(BF16)
        acc = dot(near, v_now)
        if v_before is not None:
            acc += dot(jnp.where(lower, 0.0, weights).astype(BF16), v_before)
        return top, total, acc

    def keep(h, b, top, total, acc):
        at = pl.ds(b * block, block)
        top_s[h, at, :] = jnp.broadcast_to(top, (block, width))
        total_s[h, at, :] = jnp.broadcast_to(total, (block, width))
        acc_s[h, at, :] = acc

    def near_head(h, carry):
        for b in range(blocks):
            now, before = pl.ds(b * block, block), pl.ds((b - 1) * block, block)
            q = q_buf[h, now, :]
            scores = dot_t(q, k_buf[h, now, :])
            if b:
                scores = jnp.where(lower, scores, dot_t(q, k_buf[h, before, :]))
                keep(h, b, *window(scores, v_buf[h, now, :], v_buf[h, before, :]))
            else:
                scores = jnp.where(lower, scores, NEG)
                keep(h, b, *window(scores, v_buf[h, now, :], None))
        return carry

    lax.fori_loop(0, heads // 2, near_head, 0)

    @pl.when(spot < peers - 1)
    def _():
        last = pl.ds(rows - block, block)
        lane = lax.broadcasted_iota(jnp.int32, (block, block), 1)
        stats = jnp.zeros((block, block), F32)
        for h in range(heads):
            ask(h, spot).wait_recv()
            scores = jnp.where(lower, NEG, dot_t(asked[h], k_buf[h, last, :]))
            top = jnp.max(scores, axis=1, keepdims=True)
            weights = jnp.where(lower, 0.0, jnp.exp2((scores - top) * gain))
            total = jnp.sum(weights, axis=1, keepdims=True)
            answer[h] = dot(weights.astype(BF16), v_buf[h, last, :]).astype(BF16)
            give(h, spot + 1).start()
            stats = jnp.where(lane == h, top, stats)
            stats = jnp.where(lane == slab + h, total, stats)
        stat[...] = jnp.transpose(stats)[: 2 * slab]
        give_stat(spot + 1).start()

    lax.fori_loop(heads // 2, heads, near_head, 0)

    @pl.when(spot > 0)
    def _():
        for h in range(heads):
            give(h, spot).wait_recv()
        give_stat(spot).wait_recv()

    pad = jnp.zeros((block - 2 * slab, block), F32)
    stats = jnp.transpose(jnp.concatenate([stat_back[...], pad], axis=0))
    for h in range(heads):
        at = pl.ds(0, block)
        old, new = top_s[h, at, :], stats[:, h : h + 1]
        top = jnp.maximum(old, new)
        fade, new_fade = jnp.exp2((old - top) * gain), jnp.exp2((new - top) * gain)
        top_s[h, at, :] = top
        total_s[h, at, :] = total_s[h, at, :] * fade + stats[:, slab + h : slab + h + 1] * new_fade
        acc_s[h, at, :] = acc_s[h, at, :] * fade + back[h].astype(F32) * new_fade

    def land(i, c):
        sum_copy(i, spot).wait_recv()
        return c

    lax.fori_loop(0, spot, land, 0)

    per = block // own

    def o_copy(h):
        return pltpu.make_async_copy(o_buf.at[h], o_hbm.at[h], out_sem.at[h])

    def chunk_block(h, j, b, keys, values):
        at = pl.ds(b * block, block)
        row_block = j * (block // sums) + c // sums
        scores = dot_t(q_buf[h, at, :], keys)
        scores = jnp.where(row_block < spot * blocks + b, scores, NEG)
        old = top_s[h, at, :]
        top = jnp.maximum(old, jnp.max(scores, axis=1, keepdims=True))
        weights = jnp.exp2((scores - top) * gain)
        fade = jnp.exp2((old - top) * gain)
        total = total_s[h, at, :] * fade + jnp.sum(weights, axis=1, keepdims=True)
        acc = acc_s[h, at, :] * fade + dot(weights.astype(BF16), values)
        return top, total, acc

    def far_head(h, carry):
        def rows_of(j):
            return (
                jnp.concatenate([summ[j * per + i, w, h] for i in range(per)], axis=0)
                for w in range(2)
            )

        def chunk(j, carry):
            keys, values = rows_of(j)
            for b in range(blocks):
                keep(h, b, *chunk_block(h, j, b, keys, values))
            return carry

        chunks = summ.shape[0] // per
        if chunks == 1:
            keys, values = rows_of(0)
            for b in range(blocks):
                _, total, acc = chunk_block(h, 0, b, keys, values)
                o_buf[h, pl.ds(b * block, block), :] = (acc / total).astype(BF16)
        else:
            lax.fori_loop(0, (spot * own + own - sums + block - 1) // block, chunk, 0)
            o_buf[h] = (acc_s[h] / total_s[h]).astype(BF16)
        o_copy(h).start()
        return carry

    lax.fori_loop(0, heads, far_head, 0)

    @pl.when(spot > 0)
    def _():
        for h in range(heads):
            ask(h, spot - 1).wait_send()

    @pl.when(spot < peers - 1)
    def _():
        for h in range(heads):
            give(h, spot + 1).wait_send()
        give_stat(spot + 1).wait_send()

    def sent(i, c):
        sum_copy(spot, i).wait_send()
        return c

    lax.fori_loop(spot + 1, peers, sent, 0)
    for h in range(heads):
        o_copy(h).wait()


def on_device(peers, queries, keys, values, pool_keys, pool_values):
    rows, heads, width = queries.shape
    sums, block = pool_keys.shape[1], pool_keys.shape[2]
    own = rows // block * sums
    per = block // own
    slots = -(-peers // per) * per
    q, k, v = (jnp.moveaxis(x, 1, 0) for x in (queries, keys, values))
    hbm = pl.BlockSpec(memory_space=pl.ANY)
    slab = -(-heads // 8) * 8
    out = pl.pallas_call(
        functools.partial(kernel, peers),
        out_shape=jax.ShapeDtypeStruct((heads, rows, width), BF16),
        in_specs=[hbm] * 5,
        out_specs=hbm,
        scratch_shapes=[
            pltpu.VMEM((heads, rows, width), BF16),
            pltpu.VMEM((heads, rows, width), BF16),
            pltpu.VMEM((heads, rows, width), BF16),
            pltpu.VMEM(pool_keys.shape, BF16),
            pltpu.VMEM(pool_values.shape, BF16),
            pltpu.VMEM((heads, rows, width), BF16),
            pltpu.VMEM((heads, block, width), BF16),
            pltpu.VMEM((heads, block, width), BF16),
            pltpu.VMEM((heads, block, width), BF16),
            pltpu.VMEM((2 * slab, block), F32),
            pltpu.VMEM((2 * slab, block), F32),
            pltpu.VMEM((slots, 2, heads, own, width), BF16),
            pltpu.VMEM((heads, rows, width), F32),
            pltpu.VMEM((heads, rows, width), F32),
            pltpu.VMEM((heads, rows, width), F32),
            pltpu.SemaphoreType.DMA((5,)),
            pltpu.SemaphoreType.DMA((heads,)),
            pltpu.SemaphoreType.DMA((heads,)),
            pltpu.SemaphoreType.DMA((heads,)),
            pltpu.SemaphoreType.DMA((heads,)),
            pltpu.SemaphoreType.DMA((heads,)),
            pltpu.SemaphoreType.DMA((2,)),
            pltpu.SemaphoreType.DMA((peers,)),
            pltpu.SemaphoreType.DMA((peers,)),
        ],
        compiler_params=pltpu.CompilerParams(
            collective_id=0, has_side_effects=True, vmem_limit_bytes=60 * 1024 * 1024
        ),
    )(q, k, v, pool_keys, pool_values)
    return jnp.moveaxis(out, 0, 1)


def solution(mesh):
    in_specs = (
        P(("groups", "seq"), "heads", None),
        P(("groups", "seq"), "heads", None),
        P(("groups", "seq"), "heads", None),
        P("heads", None, None),
        P("heads", None, None),
    )
    out_specs = P(("groups", "seq"), "heads", None)
    return jax.shard_map(
        functools.partial(on_device, mesh.shape["seq"]),
        mesh=mesh, in_specs=in_specs, out_specs=out_specs, check_vma=False,
    )
```

```python
import functools
import math

import jax
import jax.numpy as jnp
from jax import lax
from jax.experimental import pallas as pl
from jax.experimental.pallas import tpu as pltpu
from jax.sharding import PartitionSpec as P

NEG = -1e30
F32 = jnp.float32
BF16 = jnp.bfloat16


def dot_t(a, b):
    return lax.dot_general(a, b, (((1,), (1,)), ((), ())), preferred_element_type=F32)


def dot(a, b):
    return jnp.dot(a, b, preferred_element_type=F32)


def kernel(
    peers, q_hbm, k_hbm, v_hbm, pk_hbm, pv_hbm, o_hbm,
    q_buf, k_buf, v_buf, pk_ref, pv_ref, o_buf, asked, answer, back, stat, stat_back,
    summ, top_s, total_s, acc_s,
    in_sem, out_sem, ask_send, ask_recv, back_send, back_recv, stat_sem, sum_send, sum_recv,
):
    heads, rows, width = q_buf.shape
    sums, block = pk_ref.shape[1], pk_ref.shape[2]
    blocks = rows // block
    own = blocks * sums
    gain = (width ** -0.5) * math.log2(math.e)
    spot = lax.axis_index("seq")

    k_in = pltpu.make_async_copy(k_hbm, k_buf, in_sem.at[0])
    v_in = pltpu.make_async_copy(v_hbm, v_buf, in_sem.at[1])
    q_in = pltpu.make_async_copy(q_hbm, q_buf, in_sem.at[2])
    k_in.start()
    v_in.start()
    q_in.start()
    pk_in = pltpu.make_async_copy(pk_hbm, pk_ref, in_sem.at[3])
    pv_in = pltpu.make_async_copy(pv_hbm, pv_ref, in_sem.at[4])
    pk_in.start()
    pv_in.start()

    barrier = pltpu.get_barrier_semaphore()

    def greet(i, c):
        pl.semaphore_signal(
            barrier, inc=1, device_id={"seq": i}, device_id_type=pl.DeviceIdType.MESH
        )
        return c

    lax.fori_loop(0, spot, greet, 0)

    @pl.when(spot < peers - 1)
    def _():
        greet(spot + 1, 0)

    def clear(i, c):
        summ[:, i] = jnp.zeros((heads,) + summ.shape[2:], BF16)
        return c

    lax.fori_loop(spot + 1, summ.shape[1], clear, 0)

    @pl.when(spot == 0)
    def _():
        back[...] = jnp.zeros(back.shape, BF16)
        top_row = lax.broadcasted_iota(jnp.int32, stat_back.shape, 1) == 0
        stat_back[...] = jnp.where(top_row, NEG, 0.0)

    pl.semaphore_wait(barrier, peers - 1 - spot + jnp.where(spot > 0, 1, 0))

    def remote(src, dst, send_sem, recv_sem, to):
        return pltpu.make_async_remote_copy(
            src_ref=src,
            dst_ref=dst,
            send_sem=send_sem,
            recv_sem=recv_sem,
            device_id={"seq": to},
            device_id_type=pl.DeviceIdType.MESH,
        )

    def ask(h, to):
        src = q_hbm.at[h, pl.ds(0, block), :]
        return remote(src, asked.at[h], ask_send.at[h], ask_recv.at[h], to)

    def give(h, to):
        return remote(answer.at[h], back.at[h], back_send.at[h], back_recv.at[h], to)

    def give_stat(h, to):
        return remote(stat.at[h], stat_back.at[h], stat_sem.at[0, h], stat_sem.at[1, h], to)

    @pl.when(spot > 0)
    def _():
        for h in range(heads):
            ask(h, spot - 1).start()

    row_group = lax.broadcasted_iota(jnp.int32, (own, block), 0) // sums

    def summarise(which, pool_ref, buf, h):
        pool = pool_ref[h].astype(F32)
        tall = jnp.concatenate([pool] * blocks, axis=0)
        wide = jnp.concatenate(
            [jnp.where(row_group == b, tall, 0.0) for b in range(blocks)], axis=1
        ).astype(BF16)
        summ[h, spot, which] = dot(wide, buf[h]).astype(BF16)

    def sum_copy(h, source, to):
        at = summ.at[h, source]
        return remote(at, at, sum_send.at[h, to], sum_recv.at[h, source], to)

    k_in.wait()
    pk_in.wait()
    v_in.wait()
    pv_in.wait()
    for h in range(heads):
        summarise(0, pk_ref, k_buf, h)
        summarise(1, pv_ref, v_buf, h)

        def send(i, c):
            sum_copy(h, spot, i).start()
            return c

        lax.fori_loop(spot + 1, peers, send, 0)

    q_in.wait()

    r = lax.broadcasted_iota(jnp.int32, (block, block), 0)
    c = lax.broadcasted_iota(jnp.int32, (block, block), 1)
    lower = c <= r

    def window(scores, v_now, v_before):
        top = jnp.max(scores, axis=1, keepdims=True)
        weights = jnp.exp2((scores - top) * gain)
        total = jnp.sum(weights, axis=1, keepdims=True)
        near = jnp.where(lower, weights, 0.0).astype(BF16)
        acc = dot(near, v_now)
        if v_before is not None:
            acc += dot(jnp.where(lower, 0.0, weights).astype(BF16), v_before)
        return top, total, acc

    def keep(h, b, top, total, acc):
        at = pl.ds(b * block, block)
        top_s[h, at, :] = jnp.broadcast_to(top, (block, width))
        total_s[h, at, :] = jnp.broadcast_to(total, (block, width))
        acc_s[h, at, :] = acc

    def near_head(h, carry):
        for b in range(blocks):
            now, before = pl.ds(b * block, block), pl.ds((b - 1) * block, block)
            q = q_buf[h, now, :]
            scores = dot_t(q, k_buf[h, now, :])
            if b:
                scores = jnp.where(lower, scores, dot_t(q, k_buf[h, before, :]))
                keep(h, b, *window(scores, v_buf[h, now, :], v_buf[h, before, :]))
            else:
                scores = jnp.where(lower, scores, NEG)
                keep(h, b, *window(scores, v_buf[h, now, :], None))
        return carry

    lax.fori_loop(0, heads // 2, near_head, 0)

    @pl.when(spot < peers - 1)
    def _():
        last = pl.ds(rows - block, block)
        lane = lax.broadcasted_iota(jnp.int32, (block, block), 1)
        for h in range(heads):
            ask(h, spot).wait_recv()
            scores = jnp.where(lower, NEG, dot_t(asked[h], k_buf[h, last, :]))
            top = jnp.max(scores, axis=1, keepdims=True)
            weights = jnp.where(lower, 0.0, jnp.exp2((scores - top) * gain))
            total = jnp.sum(weights, axis=1, keepdims=True)
            answer[h] = dot(weights.astype(BF16), v_buf[h, last, :]).astype(BF16)
            give(h, spot + 1).start()
            stat[h] = jnp.transpose(jnp.where(lane == 0, top, total))[: stat.shape[1]]
            give_stat(h, spot + 1).start()

    lax.fori_loop(heads // 2, heads, near_head, 0)

    def merge(h):
        pad = jnp.zeros((block - stat.shape[1], block), F32)
        stats = jnp.transpose(jnp.concatenate([stat_back[h], pad], axis=0))
        at = pl.ds(0, block)
        old, new = top_s[h, at, :], stats[:, 0:1]
        top = jnp.maximum(old, new)
        fade, new_fade = jnp.exp2((old - top) * gain), jnp.exp2((new - top) * gain)
        top_s[h, at, :] = top
        total_s[h, at, :] = total_s[h, at, :] * fade + stats[:, 1:2] * new_fade
        acc_s[h, at, :] = acc_s[h, at, :] * fade + back[h].astype(F32) * new_fade

    per = block // own

    def o_copy(h):
        return pltpu.make_async_copy(o_buf.at[h], o_hbm.at[h], out_sem.at[h])

    key_block = lax.broadcasted_iota(jnp.int32, (rows, block), 1) // sums
    query_block = spot * blocks + lax.broadcasted_iota(jnp.int32, (rows, block), 0) // block

    def far_chunk(h, j):
        keys, values = (
            jnp.concatenate([summ[h, j * per + i, w] for i in range(per)], axis=0)
            for w in range(2)
        )
        scores = dot_t(q_buf[h], keys)
        scores = jnp.where(key_block + j * (block // sums) < query_block, scores, NEG)
        old = top_s[h]
        top = jnp.maximum(old, jnp.max(scores, axis=1, keepdims=True))
        weights = jnp.exp2((scores - top) * gain)
        fade = jnp.exp2((old - top) * gain)
        total = total_s[h] * fade + jnp.sum(weights, axis=1, keepdims=True)
        return top, total, acc_s[h] * fade + dot(weights.astype(BF16), values)

    def far_head(h, carry):
        @pl.when(spot > 0)
        def _():
            give(h, spot).wait_recv()
            give_stat(h, spot).wait_recv()

        def land(i, c):
            sum_copy(h, i, spot).wait_recv()
            return c

        lax.fori_loop(0, spot, land, 0)
        merge(h)

        def chunk(j, carry):
            top_s[h], total_s[h], acc_s[h] = far_chunk(h, j)
            return carry

        if summ.shape[1] == per:
            _, total, acc = far_chunk(h, 0)
            o_buf[h] = (acc / total).astype(BF16)
        else:
            lax.fori_loop(0, (spot * own + own - sums + block - 1) // block, chunk, 0)
            o_buf[h] = (acc_s[h] / total_s[h]).astype(BF16)
        o_copy(h).start()
        return carry

    lax.fori_loop(0, heads, far_head, 0)

    @pl.when(spot > 0)
    def _():
        for h in range(heads):
            ask(h, spot - 1).wait_send()

    @pl.when(spot < peers - 1)
    def _():
        for h in range(heads):
            give(h, spot + 1).wait_send()
            give_stat(h, spot + 1).wait_send()

    def sent(i, c):
        for h in range(heads):
            sum_copy(h, spot, i).wait_send()
        return c

    lax.fori_loop(spot + 1, peers, sent, 0)
    for h in range(heads):
        o_copy(h).wait()


def on_device(peers, queries, keys, values, pool_keys, pool_values):
    rows, heads, width = queries.shape
    sums, block = pool_keys.shape[1], pool_keys.shape[2]
    own = rows // block * sums
    per = block // own
    slots = -(-peers // per) * per
    q, k, v = (jnp.moveaxis(x, 1, 0) for x in (queries, keys, values))
    hbm = pl.BlockSpec(memory_space=pl.ANY)
    out = pl.pallas_call(
        functools.partial(kernel, peers),
        out_shape=jax.ShapeDtypeStruct((heads, rows, width), BF16),
        in_specs=[hbm] * 5,
        out_specs=hbm,
        scratch_shapes=[
            pltpu.VMEM((heads, rows, width), BF16),
            pltpu.VMEM((heads, rows, width), BF16),
            pltpu.VMEM((heads, rows, width), BF16),
            pltpu.VMEM(pool_keys.shape, BF16),
            pltpu.VMEM(pool_values.shape, BF16),
            pltpu.VMEM((heads, rows, width), BF16),
            pltpu.VMEM((heads, block, width), BF16),
            pltpu.VMEM((heads, block, width), BF16),
            pltpu.VMEM((heads, block, width), BF16),
            pltpu.VMEM((heads, 8, block), F32),
            pltpu.VMEM((heads, 8, block), F32),
            pltpu.VMEM((heads, slots, 2, own, width), BF16),
            pltpu.VMEM((heads, rows, width), F32),
            pltpu.VMEM((heads, rows, width), F32),
            pltpu.VMEM((heads, rows, width), F32),
            pltpu.SemaphoreType.DMA((5,)),
            pltpu.SemaphoreType.DMA((heads,)),
            pltpu.SemaphoreType.DMA((heads,)),
            pltpu.SemaphoreType.DMA((heads,)),
            pltpu.SemaphoreType.DMA((heads,)),
            pltpu.SemaphoreType.DMA((heads,)),
            pltpu.SemaphoreType.DMA((2, heads)),
            pltpu.SemaphoreType.DMA((heads, peers)),
            pltpu.SemaphoreType.DMA((heads, peers)),
        ],
        compiler_params=pltpu.CompilerParams(
            collective_id=0, has_side_effects=True, vmem_limit_bytes=60 * 1024 * 1024
        ),
    )(q, k, v, pool_keys, pool_values)
    return jnp.moveaxis(out, 0, 1)


def solution(mesh):
    in_specs = (
        P(("groups", "seq"), "heads", None),
        P(("groups", "seq"), "heads", None),
        P(("groups", "seq"), "heads", None),
        P("heads", None, None),
        P("heads", None, None),
    )
    out_specs = P(("groups", "seq"), "heads", None)
    return jax.shard_map(
        functools.partial(on_device, mesh.shape["seq"]),
        mesh=mesh, in_specs=in_specs, out_specs=out_specs, check_vma=False,
    )
```
